256 devices in a mesh: strip: 64 (over z, x, core), frame: 4 (over y).
Axes of the slice: x: 4, y: 4, z: 8, core: 2. Of those that a mesh axis runs over, the one named last changes fastest.
Arguments:
- frames_in: bfloat16 [4, 256, 240, 768], P('frame', 'strip'), may hold values from -6 to 6
- dw_weight: float32 [7, 7, 768], replicated, may hold values from -0.875 to 0.875
- dw_bias: float32 [768], replicated, may hold values from -4 to 4
- ln_gain: float32 [768], replicated, may hold values from 0.5 to 2
- ln_bias: float32 [768], replicated, may hold values from -3 to 3
- w_in: bfloat16 [768, 3072], replicated, may hold values from -0.21875 to 0.21875
- b_in: float32 [3072], replicated, may hold values from -3 to 3
- w_out: bfloat16 [3072, 768], replicated, may hold values from -0.109375 to 0.109375
- b_out: float32 [768], replicated, may hold values from -3 to 3
- layer_scale: float32 [768], replicated, may hold values from 0.3 to 1.5
- depth_bins: int32 [4, 256, 240], P('frame', 'strip'), may hold values from -1 to 111, as said below
- return_counts: int32 [4, 256, 240], P('frame', 'strip'), may hold values from 1 to 4
Outputs:
- features: bfloat16 [4, 256, 240, 768], P('frame', 'strip')
- probe_stat: float32 [768, 112], replicated
The draws below stay inside these ranges and needn't reach their ends.
Inputs may be any that keep to these rules, and one draw needn't show every extreme that they name: `depth_bins`: every row of every frame has at least one pixel with a return.
All inputs are finite; a program needn't handle non-finite values.
Results may differ from the reference program's by a relative error of at most 0.0056.
Values may be sent and summed in bfloat16 or wider, within the bound.
No kernel may reach another device: no remote copies, remote signals or barrier semaphores. Data moves between devices by JAX's collectives and lax.ppermute only.
A program may use at most 128 MiB of HBM per device.

```python
import math
import jax
import jax.numpy as jnp
from jax import lax

C = 768
HID = 3072
BINS = 112
KS = 7
WIDTH = 240
HEIGHT = 256
FRAMES = 4


def draw_depth_bins(key, part):
    base = jax.random.randint(jax.random.fold_in(key, 11), (FRAMES, HEIGHT, WIDTH), -1, BINS)
    column = jax.random.randint(jax.random.fold_in(key, 12), (FRAMES, HEIGHT), 0, WIDTH)
    forced = jax.random.randint(jax.random.fold_in(key, 13), (FRAMES, HEIGHT), 0, BINS)
    colpos = jnp.arange(WIDTH, dtype=jnp.int32)
    chosen = colpos[None, None, :] == column[:, :, None]
    return jnp.where(chosen, forced[:, :, None], base).astype(jnp.int32)


def draw_return_counts(key, part):
    rowpos = jnp.arange(HEIGHT, dtype=jnp.int32)
    upper = 2 + 4 * rowpos // HEIGHT
    upper = jnp.broadcast_to(upper[None, :, None], (FRAMES, HEIGHT, WIDTH))
    return jax.random.randint(key, (FRAMES, HEIGHT, WIDTH), 1, upper).astype(jnp.int32)


def steps_of(stream_key, shape, cuts, low, largest):
    gain, own = 1.0, jax.random.fold_in(stream_key, 6)
    for axis_at, blocks in cuts:
        heights = jnp.exp(jax.random.uniform(jax.random.fold_in(own, axis_at), (blocks,), jnp.float32, low / len(cuts), largest / len(cuts)))
        gain = gain * jnp.repeat(heights, shape[axis_at] // blocks).reshape([-1 if axis == axis_at else 1 for axis in range(len(shape))])
    return gain


def gaussian(own_key, dims, scale, bound, cuts=(), kind=jnp.bfloat16):
    array = jax.random.normal(own_key, dims, jnp.float32) * scale
    if len(cuts) > 0:
        array = steps_of(own_key, dims, cuts, -0.22, 0.18) * array
    return jnp.clip(array, min=-bound, max=bound).astype(kind)


def setup_inputs(seed: int = 0) -> dict:
    arg_keys = jax.random.split(jax.random.key(seed), 13)
    return {
        "frames_in": gaussian(arg_keys[0], (FRAMES, HEIGHT, WIDTH, C), 1.0, 6.0, ((0, 4), (1, 64))),
        "dw_weight": gaussian(arg_keys[1], (KS, KS, C), (KS * KS) ** -0.5, 0.875, (), jnp.float32),
        "dw_bias": gaussian(arg_keys[2], (C,), 1.0, 4.0, (), jnp.float32),
        "ln_gain": jnp.clip(jnp.exp(jax.random.uniform(arg_keys[3], (C,), jnp.float32, math.log(0.5), math.log(2.0))), 0.5, 2.0),
        "ln_bias": gaussian(arg_keys[4], (C,), 0.5, 3.0, (), jnp.float32),
        "w_in": gaussian(arg_keys[5], (C, HID), C ** -0.5, 0.21875),
        "b_in": gaussian(arg_keys[6], (HID,), 0.5, 3.0, (), jnp.float32),
        "w_out": gaussian(arg_keys[7], (HID, C), HID ** -0.5, 0.109375),
        "b_out": gaussian(arg_keys[8], (C,), 0.5, 3.0, (), jnp.float32),
        "layer_scale": jnp.clip(jnp.exp(jax.random.uniform(arg_keys[9], (C,), jnp.float32, math.log(0.3), math.log(1.5))), 0.3, 1.5),
        "depth_bins": draw_depth_bins(jax.random.fold_in(arg_keys[12], 71), 0),
        "return_counts": draw_return_counts(jax.random.fold_in(arg_keys[12], 71), 0),
    }


ridge = 0.05

def depthwise(padded, dw_weight, dw_bias, rows, cols):
    acc = jnp.zeros(padded.shape[:-3] + (rows, cols, padded.shape[-1]), jnp.float32) + dw_bias
    for a in range(7):
        for b in range(7):
            acc = acc + padded[..., a:a + rows, b:b + cols, :].astype(jnp.float32) * dw_weight[a, b]
    return acc

def block_tail(frame, conv, ln_gain, ln_bias, w_in, b_in, w_out, b_out, layer_scale):
    chans = frame.shape[-1]
    mean = lax.optimization_barrier(jnp.mean(conv, axis=-1, keepdims=True))
    centered = conv - mean
    var = lax.optimization_barrier(jnp.mean(centered * centered, axis=-1, keepdims=True))
    normed = (centered * lax.rsqrt(var + 1e-06) * ln_gain + ln_bias).astype(jnp.bfloat16)
    flat = normed.reshape(-1, chans)
    hidden = jax.nn.gelu(jnp.dot(flat.astype(jnp.float32), w_in.astype(jnp.float32), preferred_element_type=jnp.float32) + b_in, approximate=False).astype(jnp.bfloat16)
    branch = jnp.dot(hidden.astype(jnp.float32), w_out.astype(jnp.float32), preferred_element_type=jnp.float32) + b_out
    merged = frame.reshape(-1, chans).astype(jnp.float32) + layer_scale * branch
    return merged.astype(jnp.bfloat16).reshape(frame.shape)

def reference(frames_in, dw_weight, dw_bias, ln_gain, ln_bias, w_in, b_in, w_out, b_out, layer_scale, depth_bins, return_counts):

    def one_frame(carry, inputs):
        frame, bins, counts = inputs
        padded = jnp.pad(frame, ((3, 3), (3, 3), (0, 0)))
        conv = depthwise(padded, dw_weight, dw_bias, frame.shape[0], frame.shape[1])
        feats = block_tail(frame, conv, ln_gain, ln_bias, w_in, b_in, w_out, b_out, layer_scale)
        flat = feats.reshape(-1, C).astype(jnp.float32)
        bins_flat = bins.reshape(-1)
        weight = jnp.where(bins_flat >= 0, counts.reshape(-1), 0).astype(jnp.float32)
        onehot = (bins_flat[:, None] == jnp.arange(BINS, dtype=jnp.int32)[None, :]).astype(jnp.float32)
        weighted = flat * weight[:, None]
        gxx = jnp.dot(weighted.T, flat, precision=lax.Precision.HIGHEST)
        gxy = jnp.dot(weighted.T, onehot, precision=lax.Precision.HIGHEST)
        return ((carry[0] + gxx, carry[1] + gxy, carry[2] + jnp.sum(weight)), feats)
    init = (jnp.zeros((C, C), jnp.float32), jnp.zeros((C, BINS), jnp.float32), jnp.zeros((), jnp.float32))
    sums, features = lax.scan(one_frame, init, (frames_in, depth_bins, return_counts))
    total = sums[2]
    system = sums[0] / total + ridge * jnp.eye(C, dtype=jnp.float32)
    lower = jnp.linalg.cholesky(system)
    probe = jax.scipy.linalg.cho_solve((lower, True), sums[1] / total)
    return (features, probe * jnp.sqrt(total * BINS))
```

```python
import functools
import jax
import jax.numpy as jnp
from jax import lax
from jax.experimental import pallas as pl
from jax.experimental.pallas import tpu as pltpu
from jax.sharding import PartitionSpec as P

BINS = 112
C = 768
NB = C // 128
TRI = [(i, j) for i in range(NB) for j in range(i, NB)]
XY0 = len(TRI) * 128
ROWS = XY0 + C
PACK = 3584
ridge = 0.05

VMEM = pl.BlockSpec(memory_space=pltpu.VMEM)

F32 = jnp.float32
BF = jnp.bfloat16


def strip_id(z, x, c):
    return ((z % 8) * 4 + (x % 4)) * 2 + c


ALL = [(z, x, c) for z in range(8) for x in range(4) for c in range(2)]
CORE = [(strip_id(z, x, c), strip_id(z, x, 1 - c)) for z, x, c in ALL]


def x_shift(k):
    return [(strip_id(z, x, c), strip_id(z, x + k, c)) for z, x, c in ALL]


def z_flip(m):
    return [(strip_id(z, x, c), strip_id(z ^ m, x, c)) for z, x, c in ALL]


def y_shift(k):
    return [(i, (i + k) % 4) for i in range(4)]


def chunk(arr, at, size):
    return lax.dynamic_slice_in_dim(arr, at * size, size, axis=0)


def scatter4(arr, axis, pairs, me):
    size = arr.shape[0] // 4
    out = chunk(arr, me, size)
    for k in (2, 1, 3):
        out = out + lax.ppermute(chunk(arr, (me + k) % 4, size), axis, pairs(k))
    return out


def gather4(arr, axis, pairs, me):
    size = arr.shape[0]
    out = jnp.zeros((4 * size, arr.shape[1]), arr.dtype)
    got = [(k, lax.ppermute(arr, axis, pairs(k))) for k in (2, 1, 3)]
    out = lax.dynamic_update_slice_in_dim(out, arr, me * size, axis=0)
    for k, piece in got:
        out = lax.dynamic_update_slice_in_dim(out, piece, ((me + 4 - k) % 4) * size, axis=0)
    return out


def sum_devices(arr):
    strip = lax.axis_index("strip")
    y = lax.axis_index("frame")
    c = strip % 2
    x = (strip // 2) % 4
    half = arr.shape[0] // 2
    arr = chunk(arr, c, half) + lax.ppermute(chunk(arr, 1 - c, half), "strip", CORE)
    arr = scatter4(arr, "frame", y_shift, y)
    arr = scatter4(arr, "strip", x_shift, x)
    for m in (1, 2, 7):
        arr = arr + lax.ppermute(arr, "strip", z_flip(m))
    arr = gather4(arr, "strip", x_shift, x)
    arr = gather4(arr, "frame", y_shift, y)
    other = lax.ppermute(arr, "strip", CORE)
    return jnp.where(c == 0, jnp.concatenate([arr, other]), jnp.concatenate([other, arr]))


def split(v):
    hi = v.astype(BF)
    return hi, (v - hi.astype(F32)).astype(BF)


def col_sum(v):
    return jnp.sum(v, axis=0, keepdims=True)


def solve_kernel(g_ref, out_ref, a_ref, hi_ref, lo_ref, b_ref, x_ref, r_ref, d_ref, p_ref, q_ref, cat_ref):
    lane = lax.broadcasted_iota(jnp.int32, (1, 128), 1)
    total = jnp.sum(jnp.where(lane == BINS, g_ref[XY0 : XY0 + 1, :], 0.0))
    eye = jnp.where(
        lax.broadcasted_iota(jnp.int32, (128, 128), 0) == lax.broadcasted_iota(jnp.int32, (128, 128), 1), ridge, 0.0
    ).astype(F32)
    for t, (i, j) in enumerate(TRI):
        blk = g_ref[t * 128 : (t + 1) * 128, :] / total
        if i == j:
            blk = blk + eye
        ri, rj = slice(i * 128, (i + 1) * 128), slice(j * 128, (j + 1) * 128)
        a_ref[ri, rj] = blk
        hi, lo = split(blk)
        hi_ref[ri, rj] = hi
        lo_ref[ri, rj] = lo
        if i != j:
            blk = blk.T
            a_ref[rj, ri] = blk
            hi, lo = split(blk)
            hi_ref[rj, ri] = hi
            lo_ref[rj, ri] = lo
    b = jnp.where(lane < BINS, g_ref[XY0 : XY0 + C, :], 0.0) / total
    b_ref[...] = b
    r_ref[...] = b
    x_ref[...] = jnp.zeros((C, 128), F32)
    bb = col_sum(b * b)
    safe_bb = jnp.where(bb > 0, bb, 1.0)

    def inner_cond(s):
        return (s[1] > 1.0) & (s[0] < 2000)

    def rounds_cond(s):
        return (s[1] > 1.0) & (s[0] < 40)

    def rounds(s):
        n, worst = s
        r = r_ref[...]
        rr0 = col_sum(r * r)
        goal = jnp.maximum(rr0 * INNER2, bb * FINAL2 * 0.25)
        goal = jnp.where(goal > 0, goal, 1.0)
        d_ref[...] = jnp.zeros((C, 128), F32)
        p_ref[...] = r

        def inner(t):
            it, _, rr = t
            p = p_ref[...]
            hi, lo = split(p)
            cat_ref[:, :128] = hi
            cat_ref[:, 128:] = lo
            cat = cat_ref[...]
            pap = jnp.zeros((1, 128), F32)
            for m in range(3):
                rows = slice(m * 256, (m + 1) * 256)
                q = jnp.dot(hi_ref[rows, :], cat, preferred_element_type=F32) + jnp.dot(
                    lo_ref[rows, :], cat, preferred_element_type=F32
                )
                q = q[:, :128] + q[:, 128:]
                q_ref[rows, :] = q
                pap = pap + col_sum(q * p_ref[rows, :])
            alpha = jnp.where(pap > 0, rr / jnp.where(pap > 0, pap, 1.0), 0.0)
            r = r_ref[...] - alpha * q_ref[...]
            r_ref[...] = r
            d_ref[...] = d_ref[...] + alpha * p
            new = col_sum(r * r)
            beta = jnp.where(rr > 0, new / jnp.where(rr > 0, rr, 1.0), 0.0)
            p_ref[...] = r + beta * p
            return it + 1, jnp.max(new / goal), new

        DBG = lax.while_loop(inner_cond, inner, (jnp.int32(0), jnp.float32(2.0), rr0))
        x = x_ref[...] + d_ref[...]
        x_ref[...] = x
        r = b_ref[...] - jnp.dot(a_ref[...], x, preferred_element_type=F32, precision=lax.Precision.HIGHEST)
        r_ref[...] = r
        now = jnp.max(col_sum(r * r) / (safe_bb * FINAL2))
        go = (now > 1.0) & (now < 0.25 * worst)
        return n + 1, jnp.where(go, now, 0.0)

    lax.while_loop(rounds_cond, rounds, (jnp.int32(0), jnp.float32(3.0e38)))
    scale = jnp.sqrt(jnp.full((1, 128), total * BINS, F32))
    out_ref[...] = (x_ref[...] * scale)[:, :BINS]


INNER2 = 1e-7
FINAL2 = 1e-12


def solve(packed):
    mat = pltpu.VMEM((C, 128), F32)
    return pl.pallas_call(
        solve_kernel,
        out_shape=jax.ShapeDtypeStruct((C, BINS), F32),
        in_specs=[VMEM],
        out_specs=VMEM,
        scratch_shapes=[
            pltpu.VMEM((C, C), F32),
            pltpu.VMEM((C, C), BF),
            pltpu.VMEM((C, C), BF),
            mat, mat, mat, mat, mat, mat,
            pltpu.VMEM((C, 256), BF),
        ],
        compiler_params=pltpu.CompilerParams(vmem_limit_bytes=48 * 1024 * 1024),
        name="ridge_solve",
    )(packed)


def pack(xx, xy, total):
    blocks = [xx[i * 128 : (i + 1) * 128, j * 128 : (j + 1) * 128] for i, j in TRI]
    tail = jnp.zeros((C, 16), F32).at[0, 0].set(total)
    blocks.append(jnp.concatenate([xy, tail], axis=1))
    blocks.append(jnp.zeros((PACK - ROWS, 128), F32))
    return jnp.concatenate(blocks, axis=0)


def with_halo(cells, sides, width):
    for axis, dim in sides:
        count = lax.axis_size(axis)
        ends = count - 1
        head = lax.slice_in_dim(cells, 0, width, axis=dim)
        tail = lax.slice_in_dim(cells, cells.shape[dim] - width, cells.shape[dim], axis=dim)
        cells = jnp.concatenate(
            [
                lax.ppermute(tail, axis, [(i, (i + 1) % count) for i in range(ends)]),
                cells,
                lax.ppermute(head, axis, [((i + 1) % count, i) for i in range(ends)]),
            ],
            axis=dim,
        )
    return cells


def depthwise(padded, dw_weight, dw_bias, rows, cols):
    acc = jnp.zeros(padded.shape[:-3] + (rows, cols, padded.shape[-1]), jnp.float32) + dw_bias
    for a in range(7):
        for b in range(7):
            acc = (
                acc
                + padded[..., a : a + rows, b : b + cols, :].astype(jnp.float32) * dw_weight[a, b]
            )
    return acc


def block_tail(frame, conv, ln_gain, ln_bias, w_in, b_in, w_out, b_out, layer_scale):
    chans = frame.shape[-1]
    mean = jnp.mean(conv, axis=-1, keepdims=True)
    centered = conv - mean
    var = jnp.mean(centered * centered, axis=-1, keepdims=True)
    normed = (centered * lax.rsqrt(var + 1e-06) * ln_gain + ln_bias).astype(jnp.bfloat16)
    flat = normed.reshape(-1, chans)
    hidden = jax.nn.gelu(
        jnp.dot(flat, w_in, preferred_element_type=jnp.float32) + b_in, approximate=False
    ).astype(jnp.bfloat16)
    branch = jnp.dot(hidden, w_out, preferred_element_type=jnp.float32) + b_out
    merged = frame.reshape(-1, chans).astype(jnp.float32) + layer_scale * branch
    return merged.astype(jnp.bfloat16).reshape(frame.shape)


def cross_rows(left, right):
    return lax.dot_general(
        left, right, (((0,), (0,)), ((), ())), preferred_element_type=jnp.float32
    )


def per_device(
    frames_in,
    dw_weight,
    dw_bias,
    ln_gain,
    ln_bias,
    w_in,
    b_in,
    w_out,
    b_out,
    layer_scale,
    depth_bins,
    return_counts,
):
    rows = frames_in.shape[1]
    cols = frames_in.shape[2]
    chans = frames_in.shape[3]
    extended = with_halo(frames_in, (("strip", 1),), 3)
    extended = jnp.pad(extended, ((0, 0), (0, 0), (3, 3), (0, 0)))
    conv = depthwise(extended, dw_weight, dw_bias, rows, cols)
    features = block_tail(frames_in, conv, ln_gain, ln_bias, w_in, b_in, w_out, b_out, layer_scale)
    flat = features.reshape(-1, chans)
    bins_flat = depth_bins.reshape(-1)
    weight_int = jnp.where(bins_flat >= 0, return_counts.reshape(-1), 0)
    odd_weight = weight_int % 2
    even_weight = weight_int - odd_weight
    odd_rows = flat * odd_weight.astype(jnp.bfloat16)[:, None]
    even_rows = flat * even_weight.astype(jnp.bfloat16)[:, None]
    local_xx = cross_rows(odd_rows, flat) + cross_rows(even_rows, flat)
    matched = bins_flat[:, None] == jnp.arange(BINS, dtype=jnp.int32)[None, :]
    weighted_onehot = jnp.where(matched, weight_int[:, None], 0).astype(jnp.bfloat16)
    local_xy = cross_rows(flat, weighted_onehot)
    local_total = jnp.sum(weight_int.astype(jnp.float32))
    packed = sum_devices(pack(local_xx, local_xy, local_total))
    return (features, solve(packed))


def solution(mesh):
    placed = (
        P("frame", "strip", None, None),
        P(),
        P(),
        P(),
        P(),
        P(),
        P(),
        P(),
        P(),
        P(),
        P("frame", "strip", None),
        P("frame", "strip", None),
    )
    return jax.shard_map(
        per_device,
        mesh=mesh,
        in_specs=placed,
        out_specs=(P("frame", "strip", None, None), P()),
        check_vma=False,
    )
```

```python
import functools
import jax
import jax.numpy as jnp
from jax import lax
from jax.experimental import pallas as pl
from jax.experimental.pallas import tpu as pltpu
from jax.sharding import PartitionSpec as P

BINS = 112
C = 768
NB = C // 128
TRI = [(i, j) for i in range(NB) for j in range(i, NB)]
XY0 = len(TRI) * 128
ROWS = XY0 + C
PACK = 3584
ridge = 0.05

VMEM = pl.BlockSpec(memory_space=pltpu.VMEM)

F32 = jnp.float32
BF = jnp.bfloat16


def strip_id(z, x, c):
    return ((z % 8) * 4 + (x % 4)) * 2 + c


ALL = [(z, x, c) for z in range(8) for x in range(4) for c in range(2)]
CORE = [(strip_id(z, x, c), strip_id(z, x, 1 - c)) for z, x, c in ALL]


def x_shift(k):
    return [(strip_id(z, x, c), strip_id(z, x + k, c)) for z, x, c in ALL]


def z_flip(m):
    return [(strip_id(z, x, c), strip_id(z ^ m, x, c)) for z, x, c in ALL]


def y_shift(k):
    return [(i, (i + k) % 4) for i in range(4)]


def chunk(arr, at, size):
    return lax.dynamic_slice_in_dim(arr, at * size, size, axis=0)


def scatter4(arr, axis, pairs, me):
    size = arr.shape[0] // 4
    out = chunk(arr, me, size)
    for k in (2, 1, 3):
        out = out + lax.ppermute(chunk(arr, (me + k) % 4, size), axis, pairs(k))
    return out


def gather4(arr, axis, pairs, me):
    size = arr.shape[0]
    out = jnp.zeros((4 * size, arr.shape[1]), arr.dtype)
    got = [(k, lax.ppermute(arr, axis, pairs(k))) for k in (2, 1, 3)]
    out = lax.dynamic_update_slice_in_dim(out, arr, me * size, axis=0)
    for k, piece in got:
        out = lax.dynamic_update_slice_in_dim(out, piece, ((me + 4 - k) % 4) * size, axis=0)
    return out


def sum_devices(arr):
    strip = lax.axis_index("strip")
    y = lax.axis_index("frame")
    c = strip % 2
    x = (strip // 2) % 4
    half = arr.shape[0] // 2
    arr = chunk(arr, c, half) + lax.ppermute(chunk(arr, 1 - c, half), "strip", CORE)
    arr = scatter4(arr, "frame", y_shift, y)
    arr = scatter4(arr, "strip", x_shift, x)
    for m in (1, 2, 7):
        arr = arr + lax.ppermute(arr, "strip", z_flip(m))
    arr = gather4(arr, "strip", x_shift, x)
    arr = gather4(arr, "frame", y_shift, y)
    other = lax.ppermute(arr, "strip", CORE)
    return jnp.where(c == 0, jnp.concatenate([arr, other]), jnp.concatenate([other, arr]))


def split(v):
    hi = v.astype(BF)
    return hi, (v - hi.astype(F32)).astype(BF)


def col_sum(v):
    return jnp.sum(v, axis=0, keepdims=True)


def solve_kernel(g_ref, out_ref, a_ref, hi_ref, lo_ref, b_ref, x_ref, r_ref, d_ref, p_ref, q_ref, cat_ref):
    lane = lax.broadcasted_iota(jnp.int32, (1, 128), 1)
    total = jnp.max(g_ref[XY0 + BINS : XY0 + BINS + 1, :])
    eye = jnp.where(
        lax.broadcasted_iota(jnp.int32, (128, 128), 0) == lax.broadcasted_iota(jnp.int32, (128, 128), 1), ridge, 0.0
    ).astype(F32)
    for t, (i, j) in enumerate(TRI):
        blk = g_ref[t * 128 : (t + 1) * 128, :] / total
        if i == j:
            blk = blk + eye
        ri, rj = slice(i * 128, (i + 1) * 128), slice(j * 128, (j + 1) * 128)
        a_ref[ri, rj] = blk
        hi, lo = split(blk)
        hi_ref[ri, rj] = hi
        lo_ref[ri, rj] = lo
        if i != j:
            blk = blk.T
            a_ref[rj, ri] = blk
            hi, lo = split(blk)
            hi_ref[rj, ri] = hi
            lo_ref[rj, ri] = lo
    for i in range(NB):
        blk = g_ref[XY0 + i * 128 : XY0 + (i + 1) * 128, :].T / total
        b_ref[i * 128 : (i + 1) * 128, :] = jnp.where(lane < BINS, blk, 0.0)
    b = b_ref[...]
    r_ref[...] = b
    x_ref[...] = jnp.zeros((C, 128), F32)
    bb = col_sum(b * b)
    safe_bb = jnp.where(bb > 0, bb, 1.0)

    def inner_cond(s):
        return (s[1] > 1.0) & (s[0] < 2000)

    def rounds_cond(s):
        return (s[1] > 1.0) & (s[0] < 40)

    def rounds(s):
        n, worst = s
        r = r_ref[...]
        rr0 = col_sum(r * r)
        goal = jnp.maximum(rr0 * INNER2, bb * FINAL2 * 0.25)
        goal = jnp.where(goal > 0, goal, 1.0)
        d_ref[...] = jnp.zeros((C, 128), F32)
        p_ref[...] = r

        def inner(t):
            it, _, rr = t
            p = p_ref[...]
            hi, lo = split(p)
            cat_ref[:, :128] = hi
            cat_ref[:, 128:] = lo
            cat = cat_ref[...]
            pap = jnp.zeros((1, 128), F32)
            for m in range(3):
                rows = slice(m * 256, (m + 1) * 256)
                q = jnp.dot(hi_ref[rows, :], cat, preferred_element_type=F32) + jnp.dot(
                    lo_ref[rows, :], cat, preferred_element_type=F32
                )
                q = q[:, :128] + q[:, 128:]
                q_ref[rows, :] = q
                pap = pap + col_sum(q * p_ref[rows, :])
            alpha = jnp.where(pap > 0, rr / jnp.where(pap > 0, pap, 1.0), 0.0)
            r = r_ref[...] - alpha * q_ref[...]
            r_ref[...] = r
            d_ref[...] = d_ref[...] + alpha * p
            new = col_sum(r * r)
            beta = jnp.where(rr > 0, new / jnp.where(rr > 0, rr, 1.0), 0.0)
            p_ref[...] = r + beta * p
            return it + 1, jnp.max(new / goal), new

        lax.while_loop(inner_cond, inner, (jnp.int32(0), jnp.float32(2.0), rr0))
        x = x_ref[...] + d_ref[...]
        x_ref[...] = x
        r = b_ref[...] - jnp.dot(a_ref[...], x, preferred_element_type=F32, precision=lax.Precision.HIGHEST)
        r_ref[...] = r
        now = jnp.max(col_sum(r * r) / (safe_bb * FINAL2))
        go = (now > 1.0) & (now < 0.25 * worst)
        return n + 1, jnp.where(go, now, 0.0)

    lax.while_loop(rounds_cond, rounds, (jnp.int32(0), jnp.float32(3.0e38)))
    scale = jnp.sqrt(jnp.full((1, 128), total * BINS, F32))
    out_ref[...] = (x_ref[...] * scale)[:, :BINS]


INNER2 = 1e-7
FINAL2 = 1e-12


def solve(packed):
    mat = pltpu.VMEM((C, 128), F32)
    return pl.pallas_call(
        solve_kernel,
        out_shape=jax.ShapeDtypeStruct((C, BINS), F32),
        in_specs=[VMEM],
        out_specs=VMEM,
        scratch_shapes=[
            pltpu.VMEM((C, C), F32),
            pltpu.VMEM((C, C), BF),
            pltpu.VMEM((C, C), BF),
            mat, mat, mat, mat, mat, mat,
            pltpu.VMEM((C, 256), BF),
        ],
        compiler_params=pltpu.CompilerParams(vmem_limit_bytes=48 * 1024 * 1024),
        name="ridge_solve",
    )(packed)


W = 240
HID = 3072
NJ = W // 8
PJ = NJ + 6
PIX = 1024


def orders():
    p = lax.broadcasted_iota(jnp.int32, (PJ * 8, W), 0)
    w = lax.broadcasted_iota(jnp.int32, (PJ * 8, W), 1)
    spread = (w == (p % 8) * NJ + p // 8 - 3).astype(BF)
    w = lax.broadcasted_iota(jnp.int32, (W, W), 0)
    p = lax.broadcasted_iota(jnp.int32, (W, W), 1)
    back = (w == (p % 8) * NJ + p // 8).astype(BF)
    return spread, back


A1, A2, A3, A4, A5 = 0.254829592, -0.284496736, 1.421413741, -1.453152027, 1.061405429


def gelu(v):
    mag = jnp.abs(v)
    t = 1.0 / (1.0 + (0.3275911 / 2.0**0.5) * mag)
    tail = t * (0.5 * A1 + t * (0.5 * A2 + t * (0.5 * A3 + t * (0.5 * A4 + t * (0.5 * A5)))))
    return jnp.maximum(v, 0.0) - mag * tail * jnp.exp(-0.5 * (v * v))


def block_kernel(
    own, top, bot, dw, vec, b_in, spread, back, bins, counts, w_in, w_out,
    feat, packed,
    xin, xs, dwb, acc, normed, hid, f_ref, odd, even, win, wout, sems,
):
    copies = [
        pltpu.make_async_copy(own, xin.at[pl.ds(3, 4)], sems.at[0]),
        pltpu.make_async_copy(top, xin.at[pl.ds(0, 3)], sems.at[1]),
        pltpu.make_async_copy(bot, xin.at[pl.ds(7, 3)], sems.at[2]),
        pltpu.make_async_copy(w_in, win, sems.at[3]),
        pltpu.make_async_copy(w_out, wout, sems.at[4]),
    ]
    for copy in copies:
        copy.start()
    for k in range(49):
        dwb[k] = jnp.broadcast_to(dw[k : k + 1, :], (8, C))
    for copy in copies[:3]:
        copy.wait()

    def bring(r, _):
        row = jnp.dot(spread[...], xin[r], preferred_element_type=F32)
        xs[r] = row.reshape(PJ, 8, C)
        return 0

    lax.fori_loop(0, 10, bring, 0)

    def conv(t, _):
        lanes = pl.ds(pl.multiple_of((t // 5) * 128, 128), 128)
        at = (t % 5) * 6
        bias = jnp.broadcast_to(vec[0:1, lanes], (6, 8, 128))
        sums = [bias, bias, bias, bias]
        for r in range(10):
            x = xs[r, pl.ds(at, 12), :, lanes]
            for b in range(7):
                xb = x[b : b + 6]
                for h in range(4):
                    if 0 <= r - h < 7:
                        sums[h] = sums[h] + xb * dwb[(r - h) * 7 + b, :, lanes][None]
        for h in range(4):
            acc[h, pl.ds(at, 6), :, lanes] = sums[h]
        return 0

    lax.fori_loop(0, 30, conv, 0)

    def norm(h, _):
        v = acc[h].reshape(W, C)
        mean = jnp.mean(v, axis=1, keepdims=True)
        v = v - mean
        var = jnp.mean(v * v, axis=1, keepdims=True)
        v = v * lax.rsqrt(var + 1e-06) * vec[1:2, :] + vec[2:3, :]
        normed[pl.ds(pl.multiple_of(h * W, W), W), :] = v.astype(BF)
        return 0

    lax.fori_loop(0, 4, norm, 0)
    copies[3].wait()

    def up(n, _):
        cols = pl.ds(pl.multiple_of(n * 256, 256), 256)
        for m in range(4):
            rows = slice(m * W, (m + 1) * W)
            h = jnp.dot(normed[rows, :], win[:, cols], preferred_element_type=F32) + b_in[:, cols]
            hid[rows, cols] = gelu(h).astype(BF)
        return 0

    lax.fori_loop(0, HID // 256, up, 0)
    copies[4].wait()
    f_ref[4 * W :, :] = jnp.zeros((PIX - 4 * W, C), BF)

    def down(m, _):
        rows = pl.ds(pl.multiple_of(m * W, W), W)
        for n in range(3):
            cols = slice(n * 256, (n + 1) * 256)
            branch = jnp.dot(hid[rows, :], wout[:, cols], preferred_element_type=F32) + vec[3:4, cols]
            was = xs[3 + m, 3 : 3 + NJ, :, cols].reshape(W, 256)
            f_ref[rows, cols] = (was + vec[4:5, cols] * branch).astype(BF)
        feat[m] = jnp.dot(back[...], f_ref[rows, :], preferred_element_type=F32).astype(BF)
        return 0

    lax.fori_loop(0, 4, down, 0)

    weight = jnp.where(bins[...] >= 0, counts[...], 0)
    odd_w = weight % 2
    even_w = (weight - odd_w).astype(F32)
    odd_w = odd_w.astype(F32)
    for i in range(NB):
        flip = f_ref[:, i * 128 : (i + 1) * 128].astype(F32).T
        odd[...] = (flip * odd_w).astype(BF)
        even[...] = (flip * even_w).astype(BF)
        side = f_ref[:, i * 128 :]
        gram = jnp.dot(odd[...], side, preferred_element_type=F32) + jnp.dot(
            even[...], side, preferred_element_type=F32
        )
        for j in range(i, NB):
            t = TRI.index((i, j))
            packed[t * 128 : (t + 1) * 128, :] = gram[:, (j - i) * 128 : (j - i + 1) * 128]
    hot = lax.broadcasted_iota(jnp.int32, (128, PIX), 0) == bins[...]
    hot = jnp.where(hot, weight, 0).astype(F32).astype(BF)
    xy = jnp.dot(hot, f_ref[...], preferred_element_type=F32)
    total = jnp.sum(weight.astype(F32), axis=1, keepdims=True)
    xy = jnp.where(lax.broadcasted_iota(jnp.int32, (128, C), 0) == BINS, total, xy)
    for i in range(NB):
        packed[XY0 + i * 128 : XY0 + (i + 1) * 128, :] = xy[:, i * 128 : (i + 1) * 128]
    packed[ROWS:, :] = jnp.zeros((PACK - ROWS, 128), F32)


def run_block(own, top, bot, dw, vec, b_in, bins, counts, w_in, w_out):
    spread, back = orders()
    rows, cols, chans = own.shape
    anyspec = pl.BlockSpec(memory_space=pl.ANY)
    return pl.pallas_call(
        block_kernel,
        out_shape=(jax.ShapeDtypeStruct(own.shape, BF), jax.ShapeDtypeStruct((PACK, 128), F32)),
        in_specs=[anyspec] * 3 + [VMEM] * 7 + [anyspec] * 2,
        out_specs=(VMEM, VMEM),
        scratch_shapes=[
            pltpu.VMEM((10, W, C), BF),
            pltpu.VMEM((10, PJ, 8, C), F32),
            pltpu.VMEM((49, 8, C), F32),
            pltpu.VMEM((4, NJ, 8, C), F32),
            pltpu.VMEM((4 * W, C), BF),
            pltpu.VMEM((4 * W, HID), BF),
            pltpu.VMEM((PIX, C), BF),
            pltpu.VMEM((128, PIX), BF),
            pltpu.VMEM((128, PIX), BF),
            pltpu.VMEM((C, HID), BF),
            pltpu.VMEM((HID, C), BF),
            pltpu.SemaphoreType.DMA((5,)),
        ],
        compiler_params=pltpu.CompilerParams(vmem_limit_bytes=60 * 1024 * 1024),
        name="block",
    )(own, top, bot, dw, vec, b_in, spread, back, bins, counts, w_in, w_out)


def pixel_row(arr, fill):
    arr = arr.reshape(4, 8, NJ).transpose(0, 2, 1).reshape(1, 4 * W)
    return jnp.pad(arr, ((0, 0), (0, PIX - 4 * W)), constant_values=fill)


def per_device(
    frames_in, dw_weight, dw_bias, ln_gain, ln_bias, w_in, b_in, w_out, b_out, layer_scale, depth_bins, return_counts
):
    own = frames_in[0]
    ends = lax.axis_size("strip") - 1
    bot = lax.ppermute(own[:3], "strip", [(i + 1, i) for i in range(ends)])
    top = lax.ppermute(own[1:], "strip", [(i, i + 1) for i in range(ends)])
    vec = jnp.stack([dw_bias, ln_gain, ln_bias, b_out, layer_scale, b_out, b_out, b_out])
    features, packed = run_block(
        own, top, bot, dw_weight.reshape(49, C), vec, b_in.reshape(1, HID),
        pixel_row(depth_bins[0], -1), pixel_row(return_counts[0], 0), w_in, w_out,
    )
    return (features[None], solve(sum_devices(packed)))


def solution(mesh):
    placed = (
        P("frame", "strip", None, None),
        P(),
        P(),
        P(),
        P(),
        P(),
        P(),
        P(),
        P(),
        P(),
        P("frame", "strip", None),
        P("frame", "strip", None),
    )
    return jax.shard_map(
        per_device,
        mesh=mesh,
        in_specs=placed,
        out_specs=(P("frame", "strip", None, None), P()),
        check_vma=False,
    )
```

```python
import functools
import jax
import jax.numpy as jnp
from jax import lax
from jax.experimental import pallas as pl
from jax.experimental.pallas import tpu as pltpu
from jax.sharding import PartitionSpec as P

BINS = 112
C = 768
NB = C // 128
TRI = [(i, j) for i in range(NB) for j in range(i, NB)]
XY0 = len(TRI) * 128
ROWS = XY0 + C
PACK = 3584
ridge = 0.05

VMEM = pl.BlockSpec(memory_space=pltpu.VMEM)

F32 = jnp.float32
BF = jnp.bfloat16


def strip_id(z, x, c):
    return ((z % 8) * 4 + (x % 4)) * 2 + c


ALL = [(z, x, c) for z in range(8) for x in range(4) for c in range(2)]
CORE = [(strip_id(z, x, c), strip_id(z, x, 1 - c)) for z, x, c in ALL]


def x_shift(k):
    return [(strip_id(z, x, c), strip_id(z, x + k, c)) for z, x, c in ALL]


def z_flip(m):
    return [(strip_id(z, x, c), strip_id(z ^ m, x, c)) for z, x, c in ALL]


def y_shift(k):
    return [(i, (i + k) % 4) for i in range(4)]


def chunk(arr, at, size):
    return lax.dynamic_slice_in_dim(arr, at * size, size, axis=0)


def scatter4(arr, axis, pairs, me):
    size = arr.shape[0] // 4
    out = chunk(arr, me, size)
    for k in (2, 1, 3):
        out = out + lax.ppermute(chunk(arr, (me + k) % 4, size), axis, pairs(k))
    return out


def gather4(arr, axis, pairs, me):
    size = arr.shape[0]
    out = jnp.zeros((4 * size, arr.shape[1]), arr.dtype)
    got = [(k, lax.ppermute(arr, axis, pairs(k))) for k in (2, 1, 3)]
    out = lax.dynamic_update_slice_in_dim(out, arr, me * size, axis=0)
    for k, piece in got:
        out = lax.dynamic_update_slice_in_dim(out, piece, ((me + 4 - k) % 4) * size, axis=0)
    return out


def sum_devices(arr):
    strip = lax.axis_index("strip")
    y = lax.axis_index("frame")
    c = strip % 2
    x = (strip // 2) % 4
    half = arr.shape[0] // 2
    arr = chunk(arr, c, half) + lax.ppermute(chunk(arr, 1 - c, half), "strip", CORE)
    arr = scatter4(arr, "frame", y_shift, y)
    arr = scatter4(arr, "strip", x_shift, x)
    near = {m: lax.ppermute(arr, "strip", z_flip(m)) for m in (3, 2, 1)}
    arr = (arr + near[1]) + (near[2] + near[3])
    arr = arr + lax.ppermute(arr, "strip", z_flip(7))
    arr = gather4(arr, "strip", x_shift, x)
    arr = gather4(arr, "frame", y_shift, y)
    other = lax.ppermute(arr, "strip", CORE)
    return jnp.where(c == 0, jnp.concatenate([arr, other]), jnp.concatenate([other, arr]))


def split(v):
    hi = v.astype(BF)
    return hi, (v - hi.astype(F32)).astype(BF)


def split3(v):
    hi = v.astype(BF)
    rest = v - hi.astype(F32)
    lo = rest.astype(BF)
    return hi, lo, (rest - lo.astype(F32)).astype(BF)


def col_sum(v):
    return jnp.sum(v, axis=0, keepdims=True)


def solve_kernel(g_ref, out_ref, lo2_ref, hi_ref, lo_ref, b_ref, x_ref, r_ref, d_ref, p_ref, q_ref, cat_ref):
    lane = lax.broadcasted_iota(jnp.int32, (1, 128), 1)
    total = jnp.max(g_ref[XY0 + BINS : XY0 + BINS + 1, :])
    eye = jnp.where(
        lax.broadcasted_iota(jnp.int32, (128, 128), 0) == lax.broadcasted_iota(jnp.int32, (128, 128), 1), ridge, 0.0
    ).astype(F32)
    for t, (i, j) in enumerate(TRI):
        blk = g_ref[t * 128 : (t + 1) * 128, :] / total
        if i == j:
            blk = blk + eye
        ri, rj = slice(i * 128, (i + 1) * 128), slice(j * 128, (j + 1) * 128)
        hi_ref[ri, rj], lo_ref[ri, rj], lo2_ref[ri, rj] = split3(blk)
        if i != j:
            hi_ref[rj, ri], lo_ref[rj, ri], lo2_ref[rj, ri] = split3(blk.T)
    for i in range(NB):
        blk = g_ref[XY0 + i * 128 : XY0 + (i + 1) * 128, :].T / total
        b_ref[i * 128 : (i + 1) * 128, :] = jnp.where(lane < BINS, blk, 0.0)
    b = b_ref[...]
    r_ref[...] = b
    p_ref[...] = b
    x_ref[...] = jnp.zeros((C, 128), F32)
    bb = col_sum(b * b)
    safe_bb = jnp.where(bb > 0, bb, 1.0)

    def inner_cond(s):
        return (s[1] > 1.0) & (s[0] < 2000)

    def rounds_cond(s):
        return (s[1] > 1.0) & (s[0] < 40)

    def rounds(s):
        n, worst = s
        r = r_ref[...]
        rr0 = col_sum(r * r)
        goal = jnp.maximum(rr0 * INNER2, bb * FINAL2 * 0.25)
        goal = jnp.where(goal > 0, goal, 1.0)
        d_ref[...] = jnp.zeros((C, 128), F32)

        def inner(t):
            it, _, rr = t
            p = p_ref[...]
            hi, lo = split(p)
            cat_ref[:, :128] = hi
            cat_ref[:, 128:] = lo
            cat = cat_ref[...]
            pap = jnp.zeros((1, 128), F32)
            for m in range(3):
                rows = slice(m * 256, (m + 1) * 256)
                q = jnp.dot(hi_ref[rows, :], cat, preferred_element_type=F32) + jnp.dot(
                    lo_ref[rows, :], cat, preferred_element_type=F32
                )
                q = q[:, :128] + q[:, 128:]
                q_ref[rows, :] = q
                pap = pap + col_sum(q * p_ref[rows, :])
            alpha = jnp.where(pap > 0, rr / jnp.where(pap > 0, pap, 1.0), 0.0)
            r = r_ref[...] - alpha * q_ref[...]
            r_ref[...] = r
            d_ref[...] = d_ref[...] + alpha * p
            new = col_sum(r * r)
            beta = jnp.where(rr > 0, new / jnp.where(rr > 0, rr, 1.0), 0.0)
            p_ref[...] = r + beta * p
            return it + 1, jnp.max(new / goal), new

        lax.while_loop(inner_cond, inner, (jnp.int32(0), jnp.float32(2.0), rr0))
        x = x_ref[...] + d_ref[...]
        x_ref[...] = x
        hi, lo, lo2 = split3(x)
        cat_ref[:, :128] = hi
        cat_ref[:, 128:] = lo
        cat = cat_ref[...]
        for m in range(3):
            rows = slice(m * 256, (m + 1) * 256)
            q = jnp.dot(lo2_ref[rows, :], cat, preferred_element_type=F32)
            q = q + jnp.dot(lo_ref[rows, :], cat, preferred_element_type=F32)
            q = q + jnp.dot(hi_ref[rows, :], cat, preferred_element_type=F32)
            q_ref[rows, :] = q[:, :128] + (
                q[:, 128:] + jnp.dot(hi_ref[rows, :], lo2, preferred_element_type=F32)
            )
        r = b_ref[...] - q_ref[...]
        p_ref[...] = p_ref[...] + (r - r_ref[...])
        r_ref[...] = r
        now = jnp.max(col_sum(r * r) / (safe_bb * FINAL2))
        go = (now > 1.0) & (now < 0.25 * worst)
        return n + 1, jnp.where(go, now, 0.0)

    lax.while_loop(rounds_cond, rounds, (jnp.int32(0), jnp.float32(3.0e38)))
    scale = jnp.sqrt(jnp.full((1, 128), total * BINS, F32))
    out_ref[...] = (x_ref[...] * scale)[:, :BINS]


INNER2 = 1e-7
FINAL2 = 1e-12


def solve(packed):
    mat = pltpu.VMEM((C, 128), F32)
    return pl.pallas_call(
        solve_kernel,
        out_shape=jax.ShapeDtypeStruct((C, BINS), F32),
        in_specs=[VMEM],
        out_specs=VMEM,
        scratch_shapes=[
            pltpu.VMEM((C, C), BF),
            pltpu.VMEM((C, C), BF),
            pltpu.VMEM((C, C), BF),
            mat, mat, mat, mat, mat, mat,
            pltpu.VMEM((C, 256), BF),
        ],
        compiler_params=pltpu.CompilerParams(vmem_limit_bytes=48 * 1024 * 1024),
        name="ridge_solve",
    )(packed)


W = 240
HID = 3072
NJ = W // 8
PJ = NJ + 6
PIX = 1024


def orders():
    p = lax.broadcasted_iota(jnp.int32, (PJ * 8, W), 0)
    w = lax.broadcasted_iota(jnp.int32, (PJ * 8, W), 1)
    spread = (w == (p % 8) * NJ + p // 8 - 3).astype(BF)
    w = lax.broadcasted_iota(jnp.int32, (W, W), 0)
    p = lax.broadcasted_iota(jnp.int32, (W, W), 1)
    back = (w == (p % 8) * NJ + p // 8).astype(BF)
    return spread, back


ATANH_ERF = [0.7978842690838895, 0.03633414661429164, -3.302471253972585e-05, -5.527399961498717e-05, 3.974156182767768e-06, -1.3378855696121708e-07, 1.814048873178476e-09]


def gelu_half(half):
    sq = half * half
    poly = ATANH_ERF[-1] * 2.0 * 4.0 ** (len(ATANH_ERF) - 1)
    for k in range(len(ATANH_ERF) - 2, -1, -1):
        poly = poly * sq + ATANH_ERF[k] * 2.0 * 4.0**k
    return half + half * jnp.tanh(half * poly)


def spread_weights(dw, dwb):
    for k in range(49):
        dwb[k] = jnp.broadcast_to(dw[k : k + 1, :], (8, C))


def add_rows(xs, dwb, sums, at, lanes, rows):
    for slot, r in rows:
        x = xs[slot, pl.ds(at, 12), :, lanes]
        for b in range(7):
            xb = x[b : b + 6]
            for h in range(4):
                if 0 <= r - h < 7:
                    sums[h] = sums[h] + xb * dwb[(r - h) * 7 + b, :, lanes][None]
    return sums


OWN_ROWS = [(k, 3 + k) for k in range(4)]
HALO_ROWS = [(k, k if k < 3 else 4 + k) for k in range(6)]


def bring_row(r, xin, xs, spread):
    xs[r] = jnp.dot(spread[...], xin[r], preferred_element_type=F32).reshape(PJ, 8, C)


def own_kernel(own, dw, vec, spread, acc, was, xin, xs, dwb, sems):
    copy = pltpu.make_async_copy(own, xin, sems.at[0])
    copy.start()
    spread_weights(dw, dwb)
    copy.wait()

    def bring(r, _):
        bring_row(r, xin, xs, spread)
        was[pl.ds(pl.multiple_of(r * W, W), W), :] = xs[r, 3 : 3 + NJ].reshape(W, C).astype(BF)
        return 0

    lax.fori_loop(0, 4, bring, 0)

    def conv(t, _):
        lanes = pl.ds(pl.multiple_of((t // 5) * 128, 128), 128)
        at = (t % 5) * 6
        bias = jnp.broadcast_to(vec[0:1, lanes], (6, 8, 128))
        sums = add_rows(xs, dwb, [bias, bias, bias, bias], at, lanes, OWN_ROWS)
        for h in range(4):
            acc[h, pl.ds(at, 6), :, lanes] = sums[h]
        return 0

    lax.fori_loop(0, 30, conv, 0)


def block_kernel(
    part, was_in, top, bot, dw, vec, b_in, spread, back, bins, counts, w_in, w_out,
    feat, packed,
    xin, xs, dwb, acc, was, normed, hid, f_ref, odd, even, win, wout, sems,
):
    copies = [
        pltpu.make_async_copy(top, xin.at[pl.ds(0, 3)], sems.at[0]),
        pltpu.make_async_copy(bot, xin.at[pl.ds(3, 3)], sems.at[1]),
        pltpu.make_async_copy(part, acc, sems.at[2]),
        pltpu.make_async_copy(w_in, win, sems.at[3]),
        pltpu.make_async_copy(w_out, wout, sems.at[4]),
        pltpu.make_async_copy(was_in, was, sems.at[5]),
    ]
    for copy in copies:
        copy.start()
    spread_weights(dw, dwb)
    for copy in copies[:2]:
        copy.wait()

    def bring(r, _):
        bring_row(r, xin, xs, spread)
        return 0

    lax.fori_loop(0, 6, bring, 0)
    copies[2].wait()

    def conv(t, _):
        lanes = pl.ds(pl.multiple_of((t // 5) * 128, 128), 128)
        at = (t % 5) * 6
        sums = [acc[h, pl.ds(at, 6), :, lanes] for h in range(4)]
        sums = add_rows(xs, dwb, sums, at, lanes, HALO_ROWS)
        for h in range(4):
            acc[h, pl.ds(at, 6), :, lanes] = sums[h]
        return 0

    lax.fori_loop(0, 30, conv, 0)

    def norm(h, _):
        v = acc[h].reshape(W, C)
        mean = jnp.mean(v, axis=1, keepdims=True)
        v = v - mean
        var = jnp.mean(v * v, axis=1, keepdims=True)
        v = v * lax.rsqrt(var + 1e-06) * vec[1:2, :] + vec[2:3, :]
        normed[pl.ds(pl.multiple_of(h * W, W), W), :] = v.astype(BF)
        return 0

    lax.fori_loop(0, 4, norm, 0)
    copies[3].wait()

    def up(n, _):
        cols = pl.ds(pl.multiple_of(n * 256, 256), 256)
        h = jnp.dot(normed[...], win[:, cols], preferred_element_type=F32) + b_in[:, cols]
        hid[:, cols] = gelu_half(h).astype(BF)
        return 0

    lax.fori_loop(0, HID // 256, up, 0)
    copies[4].wait()
    copies[5].wait()
    f_ref[4 * W :, :] = jnp.zeros((PIX - 4 * W, C), BF)

    def down(n, _):
        cols = pl.ds(pl.multiple_of(n * 256, 256), 256)
        branch = jnp.dot(hid[...], wout[:, cols], preferred_element_type=F32) + vec[3:4, cols]
        f_ref[: 4 * W, cols] = (was[:, cols].astype(F32) + vec[4:5, cols] * branch).astype(BF)
        return 0

    lax.fori_loop(0, C // 256, down, 0)

    def order(m, _):
        rows = pl.ds(pl.multiple_of(m * W, W), W)
        feat[m] = jnp.dot(back[...], f_ref[rows, :], preferred_element_type=F32).astype(BF)
        return 0

    lax.fori_loop(0, 4, order, 0)

    weight = jnp.where(bins[...] >= 0, counts[...], 0)
    odd_w = weight % 2
    even_w = (weight - odd_w).astype(F32)
    odd_w = odd_w.astype(F32)
    for i in range(NB):
        flip = f_ref[:, i * 128 : (i + 1) * 128].astype(F32).T
        odd[...] = (flip * odd_w).astype(BF)
        even[...] = (flip * even_w).astype(BF)
        side = f_ref[:, i * 128 :]
        gram = jnp.dot(odd[...], side, preferred_element_type=F32) + jnp.dot(
            even[...], side, preferred_element_type=F32
        )
        for j in range(i, NB):
            t = TRI.index((i, j))
            packed[t * 128 : (t + 1) * 128, :] = gram[:, (j - i) * 128 : (j - i + 1) * 128]
    hot = lax.broadcasted_iota(jnp.int32, (128, PIX), 0) == bins[...]
    hot = jnp.where(hot, weight, 0).astype(F32).astype(BF)
    xy = jnp.dot(hot, f_ref[...], preferred_element_type=F32)
    total = jnp.sum(weight.astype(F32), axis=1, keepdims=True)
    xy = jnp.where(lax.broadcasted_iota(jnp.int32, (128, C), 0) == BINS, total, xy)
    for i in range(NB):
        packed[XY0 + i * 128 : XY0 + (i + 1) * 128, :] = xy[:, i * 128 : (i + 1) * 128]
    packed[ROWS:, :] = jnp.zeros((PACK - ROWS, 128), F32)


def run_own(own, dw, vec, spread):
    part = jax.ShapeDtypeStruct((4, NJ, 8, C), F32)
    was = jax.ShapeDtypeStruct((4 * W, C), BF)
    return pl.pallas_call(
        own_kernel,
        out_shape=(part, was),
        in_specs=[pl.BlockSpec(memory_space=pl.ANY)] + [VMEM] * 3,
        out_specs=(VMEM, VMEM),
        scratch_shapes=[
            pltpu.VMEM((4, W, C), BF),
            pltpu.VMEM((4, PJ, 8, C), F32),
            pltpu.VMEM((49, 8, C), F32),
            pltpu.SemaphoreType.DMA((1,)),
        ],
        compiler_params=pltpu.CompilerParams(vmem_limit_bytes=24 * 1024 * 1024),
        cost_estimate=pl.CostEstimate(flops=6_000_000_000, bytes_accessed=12_000_000, transcendentals=0),
        name="own_rows",
    )(own, dw, vec, spread)


def run_block(own, top, bot, dw, vec, b_in, bins, counts, w_in, w_out):
    spread, back = orders()
    part, was = run_own(own, dw, vec, spread)
    anyspec = pl.BlockSpec(memory_space=pl.ANY)
    return pl.pallas_call(
        block_kernel,
        out_shape=(jax.ShapeDtypeStruct(own.shape, BF), jax.ShapeDtypeStruct((PACK, 128), F32)),
        in_specs=[anyspec] * 4 + [VMEM] * 7 + [anyspec] * 2,
        out_specs=(VMEM, VMEM),
        scratch_shapes=[
            pltpu.VMEM((6, W, C), BF),
            pltpu.VMEM((6, PJ, 8, C), F32),
            pltpu.VMEM((49, 8, C), F32),
            pltpu.VMEM((4, NJ, 8, C), F32),
            pltpu.VMEM((4 * W, C), BF),
            pltpu.VMEM((4 * W, C), BF),
            pltpu.VMEM((4 * W, HID), BF),
            pltpu.VMEM((PIX, C), BF),
            pltpu.VMEM((128, PIX), BF),
            pltpu.VMEM((128, PIX), BF),
            pltpu.VMEM((C, HID), BF),
            pltpu.VMEM((HID, C), BF),
            pltpu.SemaphoreType.DMA((6,)),
        ],
        compiler_params=pltpu.CompilerParams(vmem_limit_bytes=48 * 1024 * 1024),
        name="block",
    )(part, was, top, bot, dw, vec, b_in, spread, back, bins, counts, w_in, w_out)


def pixel_row(arr, fill):
    arr = arr.reshape(4, 8, NJ).transpose(0, 2, 1).reshape(1, 4 * W)
    return jnp.pad(arr, ((0, 0), (0, PIX - 4 * W)), constant_values=fill)


def per_device(
    frames_in, dw_weight, dw_bias, ln_gain, ln_bias, w_in, b_in, w_out, b_out, layer_scale, depth_bins, return_counts
):
    own = frames_in[0]
    ends = lax.axis_size("strip") - 1
    bot = lax.ppermute(own[:3], "strip", [(i + 1, i) for i in range(ends)])
    top = lax.ppermute(own[1:], "strip", [(i, i + 1) for i in range(ends)])
    vec = jnp.stack([dw_bias, 0.5 * ln_gain, 0.5 * ln_bias, b_out, layer_scale, b_out, b_out, b_out])
    features, packed = run_block(
        own, top, bot, dw_weight.reshape(49, C), vec, 0.5 * b_in.reshape(1, HID),
        pixel_row(depth_bins[0], -1), pixel_row(return_counts[0], 0), w_in, w_out,
    )
    return (features[None], solve(sum_devices(packed)))


def solution(mesh):
    placed = (
        P("frame", "strip", None, None),
        P(),
        P(),
        P(),
        P(),
        P(),
        P(),
        P(),
        P(),
        P(),
        P("frame", "strip", None),
        P("frame", "strip", None),
    )
    return jax.shard_map(
        per_device,
        mesh=mesh,
        in_specs=placed,
        out_specs=(P("frame", "strip", None, None), P()),
        check_vma=False,
    )
```

```python
import functools
import jax
import jax.numpy as jnp
from jax import lax
from jax.experimental import pallas as pl
from jax.experimental.pallas import tpu as pltpu
from jax.sharding import PartitionSpec as P

BINS = 112
C = 768
NB = C // 128
TRI = [(i, j) for i in range(NB) for j in range(i, NB)]
XY0 = len(TRI) * 128
ROWS = XY0 + C
PACK = 3584
ridge = 0.05

VMEM = pl.BlockSpec(memory_space=pltpu.VMEM)

F32 = jnp.float32
BF = jnp.bfloat16


def strip_id(z, x, c):
    return ((z % 8) * 4 + (x % 4)) * 2 + c


ALL = [(z, x, c) for z in range(8) for x in range(4) for c in range(2)]
CORE = [(strip_id(z, x, c), strip_id(z, x, 1 - c)) for z, x, c in ALL]


def x_shift(k):
    return [(strip_id(z, x, c), strip_id(z, x + k, c)) for z, x, c in ALL]


def z_flip(m):
    return [(strip_id(z, x, c), strip_id(z ^ m, x, c)) for z, x, c in ALL]


def y_shift(k):
    return [(i, (i + k) % 4) for i in range(4)]


def chunk(arr, at, size):
    return lax.dynamic_slice_in_dim(arr, at * size, size, axis=0)


def scatter4(arr, axis, pairs, me):
    size = arr.shape[0] // 4
    out = chunk(arr, me, size)
    for k in (2, 1, 3):
        out = out + lax.ppermute(chunk(arr, (me + k) % 4, size), axis, pairs(k))
    return out


def gather4(arr, axis, pairs, me):
    size = arr.shape[0]
    out = jnp.zeros((4 * size, arr.shape[1]), arr.dtype)
    got = [(k, lax.ppermute(arr, axis, pairs(k))) for k in (2, 1, 3)]
    out = lax.dynamic_update_slice_in_dim(out, arr, me * size, axis=0)
    for k, piece in got:
        out = lax.dynamic_update_slice_in_dim(out, piece, ((me + 4 - k) % 4) * size, axis=0)
    return out


def sum_devices(arr):
    strip = lax.axis_index("strip")
    y = lax.axis_index("frame")
    c = strip % 2
    x = (strip // 2) % 4
    half = arr.shape[0] // 2
    arr = chunk(arr, c, half) + lax.ppermute(chunk(arr, 1 - c, half), "strip", CORE)
    arr = scatter4(arr, "frame", y_shift, y)
    arr = scatter4(arr, "strip", x_shift, x)
    near = {m: lax.ppermute(arr, "strip", z_flip(m)) for m in (3, 2, 1)}
    arr = (arr + near[1]) + (near[2] + near[3])
    arr = arr + lax.ppermute(arr, "strip", z_flip(7))
    arr = gather4(arr, "strip", x_shift, x)
    arr = gather4(arr, "frame", y_shift, y)
    other = lax.ppermute(arr, "strip", CORE)
    return jnp.where(c == 0, jnp.concatenate([arr, other]), jnp.concatenate([other, arr]))


def split(v):
    hi = v.astype(BF)
    return hi, (v - hi.astype(F32)).astype(BF)


def split3(v):
    hi = v.astype(BF)
    rest = v - hi.astype(F32)
    lo = rest.astype(BF)
    return hi, lo, (rest - lo.astype(F32)).astype(BF)


def col_sum(v):
    return jnp.sum(v, axis=0, keepdims=True)


def solve_kernel(g_ref, out_ref, lo2_ref, hi_ref, lo_ref, b_ref, x_ref, r_ref, d_ref, p_ref, q_ref, cat_ref):
    lane = lax.broadcasted_iota(jnp.int32, (1, 128), 1)
    total = jnp.max(g_ref[XY0 + BINS : XY0 + BINS + 1, :])
    eye = jnp.where(
        lax.broadcasted_iota(jnp.int32, (128, 128), 0) == lax.broadcasted_iota(jnp.int32, (128, 128), 1), ridge, 0.0
    ).astype(F32)
    for t, (i, j) in enumerate(TRI):
        blk = g_ref[t * 128 : (t + 1) * 128, :] / total
        if i == j:
            blk = blk + eye
        ri, rj = slice(i * 128, (i + 1) * 128), slice(j * 128, (j + 1) * 128)
        hi_ref[ri, rj], lo_ref[ri, rj], lo2_ref[ri, rj] = split3(blk)
        if i != j:
            hi_ref[rj, ri], lo_ref[rj, ri], lo2_ref[rj, ri] = split3(blk.T)
    for i in range(NB):
        blk = g_ref[XY0 + i * 128 : XY0 + (i + 1) * 128, :].T / total
        b_ref[i * 128 : (i + 1) * 128, :] = jnp.where(lane < BINS, blk, 0.0)
    b = b_ref[...]
    r_ref[...] = b
    x_ref[...] = jnp.zeros((C, 128), F32)
    bb = col_sum(b * b)
    safe_bb = jnp.where(bb > 0, bb, 1.0)

    def inner_cond(s):
        return (s[1] > 1.0) & (s[0] < 2000)

    def rounds_cond(s):
        return (s[1] > 1.0) & (s[0] < 40)

    def rounds(s):
        n, worst = s
        r = r_ref[...]
        rr0 = col_sum(r * r)
        goal = jnp.maximum(rr0 * INNER2, bb * FINAL2 * 0.25)
        goal = jnp.where(goal > 0, goal, 1.0)
        d_ref[...] = jnp.zeros((C, 128), F32)
        p_ref[...] = r

        def inner(t):
            it, _, rr = t
            p = p_ref[...]
            hi, lo = split(p)
            cat_ref[:, :128] = hi
            cat_ref[:, 128:] = lo
            cat = cat_ref[...]
            pap = jnp.zeros((1, 128), F32)
            for m in range(2):
                rows = slice(m * 384, (m + 1) * 384)
                q = jnp.dot(hi_ref[rows, :], cat, preferred_element_type=F32) + jnp.dot(
                    lo_ref[rows, :], cat, preferred_element_type=F32
                )
                q = q[:, :128] + q[:, 128:]
                q_ref[rows, :] = q
                pap = pap + col_sum(q * p_ref[rows, :])
            alpha = jnp.where(pap > 0, rr / jnp.where(pap > 0, pap, 1.0), 0.0)
            r = r_ref[...] - alpha * q_ref[...]
            r_ref[...] = r
            d_ref[...] = d_ref[...] + alpha * p
            new = col_sum(r * r)
            beta = jnp.where(rr > 0, new / jnp.where(rr > 0, rr, 1.0), 0.0)
            p_ref[...] = r + beta * p
            return it + 1, jnp.max(new / goal), new

        lax.while_loop(inner_cond, inner, (jnp.int32(0), jnp.float32(2.0), rr0))
        x = x_ref[...] + d_ref[...]
        x_ref[...] = x
        hi, lo, lo2 = split3(x)
        cat_ref[:, :128] = hi
        cat_ref[:, 128:] = lo
        cat = cat_ref[...]
        for m in range(3):
            rows = slice(m * 256, (m + 1) * 256)
            q = jnp.dot(lo2_ref[rows, :], cat, preferred_element_type=F32)
            q = q + jnp.dot(lo_ref[rows, :], cat, preferred_element_type=F32)
            q = q + jnp.dot(hi_ref[rows, :], cat, preferred_element_type=F32)
            q_ref[rows, :] = q[:, :128] + (
                q[:, 128:] + jnp.dot(hi_ref[rows, :], lo2, preferred_element_type=F32)
            )
        r = b_ref[...] - q_ref[...]
        r_ref[...] = r
        now = jnp.max(col_sum(r * r) / (safe_bb * FINAL2))
        go = (now > 1.0) & (now < 0.25 * worst)
        return n + 1, jnp.where(go, now, 0.0)

    lax.while_loop(rounds_cond, rounds, (jnp.int32(0), jnp.float32(3.0e38)))
    scale = jnp.sqrt(jnp.full((1, 128), total * BINS, F32))
    out_ref[...] = (x_ref[...] * scale)[:, :BINS]


INNER2 = 1e-8
FINAL2 = 1e-12


def solve(packed):
    mat = pltpu.VMEM((C, 128), F32)
    return pl.pallas_call(
        solve_kernel,
        out_shape=jax.ShapeDtypeStruct((C, BINS), F32),
        in_specs=[VMEM],
        out_specs=VMEM,
        scratch_shapes=[
            pltpu.VMEM((C, C), BF),
            pltpu.VMEM((C, C), BF),
            pltpu.VMEM((C, C), BF),
            mat, mat, mat, mat, mat, mat,
            pltpu.VMEM((C, 256), BF),
        ],
        compiler_params=pltpu.CompilerParams(vmem_limit_bytes=48 * 1024 * 1024),
        name="ridge_solve",
    )(packed)


W = 240
HID = 3072
NJ = W // 8
PJ = NJ + 6
PIX = 1024


def orders():
    p = lax.broadcasted_iota(jnp.int32, (PJ * 8, W), 0)
    w = lax.broadcasted_iota(jnp.int32, (PJ * 8, W), 1)
    spread = (w == (p % 8) * NJ + p // 8 - 3).astype(BF)
    w = lax.broadcasted_iota(jnp.int32, (W, W), 0)
    p = lax.broadcasted_iota(jnp.int32, (W, W), 1)
    back = (w == (p % 8) * NJ + p // 8).astype(BF)
    return spread, back


ATANH_ERF = [0.7978842690838895, 0.03633414661429164, -3.302471253972585e-05, -5.527399961498717e-05, 3.974156182767768e-06, -1.3378855696121708e-07, 1.814048873178476e-09]


def gelu_half(half):
    sq = half * half
    poly = ATANH_ERF[-1] * 2.0 * 4.0 ** (len(ATANH_ERF) - 1)
    for k in range(len(ATANH_ERF) - 2, -1, -1):
        poly = poly * sq + ATANH_ERF[k] * 2.0 * 4.0**k
    return half + half * jnp.tanh(half * poly)


def spread_weights(dw, dwb):
    for k in range(49):
        dwb[k] = jnp.broadcast_to(dw[k : k + 1, :], (8, C))


def add_rows(xs, dwb, sums, at, lanes, rows):
    for slot, r in rows:
        x = xs[slot, pl.ds(at, 12), :, lanes]
        for b in range(7):
            xb = x[b : b + 6]
            for h in range(4):
                if 0 <= r - h < 7:
                    sums[h] = sums[h] + xb * dwb[(r - h) * 7 + b, :, lanes][None]
    return sums


OWN_ROWS = [(k, 3 + k) for k in range(4)]
HALO_ROWS = [(k, k if k < 3 else 4 + k) for k in range(6)]


def bring_row(r, xin, xs, spread):
    xs[r] = jnp.dot(spread[...], xin[r], preferred_element_type=F32).reshape(PJ, 8, C)


def own_kernel(own, dw, vec, spread, acc, was, xin, xs, dwb, sems):
    copy = pltpu.make_async_copy(own, xin, sems.at[0])
    copy.start()
    spread_weights(dw, dwb)
    copy.wait()

    def bring(r, _):
        bring_row(r, xin, xs, spread)
        was[pl.ds(pl.multiple_of(r * W, W), W), :] = xs[r, 3 : 3 + NJ].reshape(W, C).astype(BF)
        return 0

    lax.fori_loop(0, 4, bring, 0)

    def conv(t, _):
        lanes = pl.ds(pl.multiple_of((t // 5) * 128, 128), 128)
        at = (t % 5) * 6
        bias = jnp.broadcast_to(vec[0:1, lanes], (6, 8, 128))
        sums = add_rows(xs, dwb, [bias, bias, bias, bias], at, lanes, OWN_ROWS)
        for h in range(4):
            acc[h, pl.ds(at, 6), :, lanes] = sums[h]
        return 0

    lax.fori_loop(0, 30, conv, 0)


def block_kernel(
    part, was_in, top, bot, dw, vec, b_in, spread, back, bins, counts, w_in, w_out,
    feat, packed,
    xin, xs, dwb, acc, was, normed, hid, f_ref, odd, even, win, wout, sems,
):
    copies = [
        pltpu.make_async_copy(top, xin.at[pl.ds(0, 3)], sems.at[0]),
        pltpu.make_async_copy(bot, xin.at[pl.ds(3, 3)], sems.at[1]),
        pltpu.make_async_copy(part, acc, sems.at[2]),
        pltpu.make_async_copy(w_in, win, sems.at[3]),
        pltpu.make_async_copy(w_out, wout, sems.at[4]),
        pltpu.make_async_copy(was_in, was, sems.at[5]),
    ]
    for copy in copies:
        copy.start()
    spread_weights(dw, dwb)
    for copy in copies[:2]:
        copy.wait()

    def bring(r, _):
        bring_row(r, xin, xs, spread)
        return 0

    lax.fori_loop(0, 6, bring, 0)
    copies[2].wait()

    def conv(t, _):
        lanes = pl.ds(pl.multiple_of((t // 5) * 128, 128), 128)
        at = (t % 5) * 6
        sums = [acc[h, pl.ds(at, 6), :, lanes] for h in range(4)]
        sums = add_rows(xs, dwb, sums, at, lanes, HALO_ROWS)
        for h in range(4):
            acc[h, pl.ds(at, 6), :, lanes] = sums[h]
        return 0

    lax.fori_loop(0, 30, conv, 0)

    def norm(h, _):
        v = acc[h].reshape(W, C)
        mean = jnp.mean(v, axis=1, keepdims=True)
        v = v - mean
        var = jnp.mean(v * v, axis=1, keepdims=True)
        v = v * lax.rsqrt(var + 1e-06) * vec[1:2, :] + vec[2:3, :]
        normed[pl.ds(pl.multiple_of(h * W, W), W), :] = v.astype(BF)
        return 0

    lax.fori_loop(0, 4, norm, 0)
    copies[3].wait()

    def up(n, _):
        cols = pl.ds(pl.multiple_of(n * 256, 256), 256)
        h = jnp.dot(normed[...], win[:, cols], preferred_element_type=F32) + b_in[:, cols]
        hid[:, cols] = gelu_half(h).astype(BF)
        return 0

    lax.fori_loop(0, HID // 256, up, 0)
    copies[4].wait()
    copies[5].wait()
    f_ref[4 * W :, :] = jnp.zeros((PIX - 4 * W, C), BF)

    def down(n, _):
        cols = pl.ds(pl.multiple_of(n * 256, 256), 256)
        branch = jnp.dot(hid[...], wout[:, cols], preferred_element_type=F32) + vec[3:4, cols]
        f_ref[: 4 * W, cols] = (was[:, cols].astype(F32) + vec[4:5, cols] * branch).astype(BF)
        return 0

    lax.fori_loop(0, C // 256, down, 0)

    def order(m, _):
        rows = pl.ds(pl.multiple_of(m * W, W), W)
        feat[m] = jnp.dot(back[...], f_ref[rows, :], preferred_element_type=F32).astype(BF)
        return 0

    lax.fori_loop(0, 4, order, 0)

    weight = jnp.where(bins[...] >= 0, counts[...], 0)
    odd_w = weight % 2
    even_w = (weight - odd_w).astype(F32)
    odd_w = odd_w.astype(F32)
    for i in range(NB):
        flip = f_ref[:, i * 128 : (i + 1) * 128].astype(F32).T
        odd[...] = (flip * odd_w).astype(BF)
        even[...] = (flip * even_w).astype(BF)
        side = f_ref[:, i * 128 :]
        gram = jnp.dot(odd[...], side, preferred_element_type=F32) + jnp.dot(
            even[...], side, preferred_element_type=F32
        )
        for j in range(i, NB):
            t = TRI.index((i, j))
            packed[t * 128 : (t + 1) * 128, :] = gram[:, (j - i) * 128 : (j - i + 1) * 128]
    hot = lax.broadcasted_iota(jnp.int32, (128, PIX), 0) == bins[...]
    hot = jnp.where(hot, weight, 0).astype(F32).astype(BF)
    xy = jnp.dot(hot, f_ref[...], preferred_element_type=F32)
    total = jnp.sum(weight.astype(F32), axis=1, keepdims=True)
    xy = jnp.where(lax.broadcasted_iota(jnp.int32, (128, C), 0) == BINS, total, xy)
    for i in range(NB):
        packed[XY0 + i * 128 : XY0 + (i + 1) * 128, :] = xy[:, i * 128 : (i + 1) * 128]
    packed[ROWS:, :] = jnp.zeros((PACK - ROWS, 128), F32)


def run_own(own, dw, vec, spread):
    part = jax.ShapeDtypeStruct((4, NJ, 8, C), F32)
    was = jax.ShapeDtypeStruct((4 * W, C), BF)
    return pl.pallas_call(
        own_kernel,
        out_shape=(part, was),
        in_specs=[pl.BlockSpec(memory_space=pl.ANY)] + [VMEM] * 3,
        out_specs=(VMEM, VMEM),
        scratch_shapes=[
            pltpu.VMEM((4, W, C), BF),
            pltpu.VMEM((4, PJ, 8, C), F32),
            pltpu.VMEM((49, 8, C), F32),
            pltpu.SemaphoreType.DMA((1,)),
        ],
        compiler_params=pltpu.CompilerParams(vmem_limit_bytes=24 * 1024 * 1024),
        cost_estimate=pl.CostEstimate(flops=6_000_000_000, bytes_accessed=12_000_000, transcendentals=0),
        name="own_rows",
    )(own, dw, vec, spread)


def run_block(own, top, bot, dw, vec, b_in, bins, counts, w_in, w_out):
    spread, back = orders()
    part, was = run_own(own, dw, vec, spread)
    anyspec = pl.BlockSpec(memory_space=pl.ANY)
    return pl.pallas_call(
        block_kernel,
        out_shape=(jax.ShapeDtypeStruct(own.shape, BF), jax.ShapeDtypeStruct((PACK, 128), F32)),
        in_specs=[anyspec] * 4 + [VMEM] * 7 + [anyspec] * 2,
        out_specs=(VMEM, VMEM),
        scratch_shapes=[
            pltpu.VMEM((6, W, C), BF),
            pltpu.VMEM((6, PJ, 8, C), F32),
            pltpu.VMEM((49, 8, C), F32),
            pltpu.VMEM((4, NJ, 8, C), F32),
            pltpu.VMEM((4 * W, C), BF),
            pltpu.VMEM((4 * W, C), BF),
            pltpu.VMEM((4 * W, HID), BF),
            pltpu.VMEM((PIX, C), BF),
            pltpu.VMEM((128, PIX), BF),
            pltpu.VMEM((128, PIX), BF),
            pltpu.VMEM((C, HID), BF),
            pltpu.VMEM((HID, C), BF),
            pltpu.SemaphoreType.DMA((6,)),
        ],
        compiler_params=pltpu.CompilerParams(vmem_limit_bytes=48 * 1024 * 1024),
        name="block",
    )(part, was, top, bot, dw, vec, b_in, spread, back, bins, counts, w_in, w_out)


def pixel_row(arr, fill):
    arr = arr.reshape(4, 8, NJ).transpose(0, 2, 1).reshape(1, 4 * W)
    return jnp.pad(arr, ((0, 0), (0, PIX - 4 * W)), constant_values=fill)


def per_device(
    frames_in, dw_weight, dw_bias, ln_gain, ln_bias, w_in, b_in, w_out, b_out, layer_scale, depth_bins, return_counts
):
    own = frames_in[0]
    ends = lax.axis_size("strip") - 1
    bot = lax.ppermute(own[:3], "strip", [(i + 1, i) for i in range(ends)])
    top = lax.ppermute(own[1:], "strip", [(i, i + 1) for i in range(ends)])
    vec = jnp.stack([dw_bias, 0.5 * ln_gain, 0.5 * ln_bias, b_out, layer_scale, b_out, b_out, b_out])
    features, packed = run_block(
        own, top, bot, dw_weight.reshape(49, C), vec, 0.5 * b_in.reshape(1, HID),
        pixel_row(depth_bins[0], -1), pixel_row(return_counts[0], 0), w_in, w_out,
    )
    return (features[None], solve(sum_devices(packed)))


def solution(mesh):
    placed = (
        P("frame", "strip", None, None),
        P(),
        P(),
        P(),
        P(),
        P(),
        P(),
        P(),
        P(),
        P(),
        P("frame", "strip", None),
        P("frame", "strip", None),
    )
    return jax.shard_map(
        per_device,
        mesh=mesh,
        in_specs=placed,
        out_specs=(P("frame", "strip", None, None), P()),
        check_vma=False,
    )
```

```python
import functools
import jax
import jax.numpy as jnp
from jax import lax
from jax.experimental import pallas as pl
from jax.experimental.pallas import tpu as pltpu
from jax.sharding import PartitionSpec as P

BINS = 112
C = 768
NB = C // 128
TRI = [(i, j) for i in range(NB) for j in range(i, NB)]
XY0 = len(TRI) * 128
ROWS = XY0 + C
PACK = 3584
ridge = 0.05

VMEM = pl.BlockSpec(memory_space=pltpu.VMEM)

F32 = jnp.float32
BF = jnp.bfloat16


def strip_id(z, x, c):
    return ((z % 8) * 4 + (x % 4)) * 2 + c


ALL = [(z, x, c) for z in range(8) for x in range(4) for c in range(2)]
CORE = [(strip_id(z, x, c), strip_id(z, x, 1 - c)) for z, x, c in ALL]


def x_shift(k):
    return [(strip_id(z, x, c), strip_id(z, x + k, c)) for z, x, c in ALL]


def z_flip(m):
    return [(strip_id(z, x, c), strip_id(z ^ m, x, c)) for z, x, c in ALL]


def y_shift(k):
    return [(i, (i + k) % 4) for i in range(4)]


def chunk(arr, at, size):
    return lax.dynamic_slice_in_dim(arr, at * size, size, axis=0)


def scatter4(arr, axis, pairs, me):
    size = arr.shape[0] // 4
    out = chunk(arr, me, size)
    for k in (2, 1, 3):
        out = out + lax.ppermute(chunk(arr, (me + k) % 4, size), axis, pairs(k))
    return out


def gather4(arr, axis, pairs, me):
    size = arr.shape[0]
    out = jnp.zeros((4 * size, arr.shape[1]), arr.dtype)
    got = [(k, lax.ppermute(arr, axis, pairs(k))) for k in (2, 1, 3)]
    out = lax.dynamic_update_slice_in_dim(out, arr, me * size, axis=0)
    for k, piece in got:
        out = lax.dynamic_update_slice_in_dim(out, piece, ((me + 4 - k) % 4) * size, axis=0)
    return out


def sum_devices(arr):
    strip = lax.axis_index("strip")
    y = lax.axis_index("frame")
    c = strip % 2
    x = (strip // 2) % 4
    half = arr.shape[0] // 2
    arr = chunk(arr, c, half) + lax.ppermute(chunk(arr, 1 - c, half), "strip", CORE)
    arr = scatter4(arr, "frame", y_shift, y)
    arr = scatter4(arr, "strip", x_shift, x)
    near = {m: lax.ppermute(arr, "strip", z_flip(m)) for m in (3, 2, 1)}
    arr = (arr + near[1]) + (near[2] + near[3])
    arr = arr + lax.ppermute(arr, "strip", z_flip(7))
    arr = gather4(arr, "strip", x_shift, x)
    arr = gather4(arr, "frame", y_shift, y)
    other = lax.ppermute(arr, "strip", CORE)
    return jnp.where(c == 0, jnp.concatenate([arr, other]), jnp.concatenate([other, arr]))


def split(v):
    hi = v.astype(BF)
    return hi, (v - hi.astype(F32)).astype(BF)


def split3(v):
    hi = v.astype(BF)
    rest = v - hi.astype(F32)
    lo = rest.astype(BF)
    return hi, lo, (rest - lo.astype(F32)).astype(BF)


def col_sum(v):
    return jnp.sum(v, axis=0, keepdims=True)


def solve_kernel(g_ref, out_ref, lo2_ref, hi_ref, lo_ref, b_ref, x_ref, r_ref, d_ref, p_ref, q_ref, cat_ref):
    lane = lax.broadcasted_iota(jnp.int32, (1, 128), 1)
    total = jnp.max(g_ref[XY0 + BINS : XY0 + BINS + 1, :])
    eye = jnp.where(
        lax.broadcasted_iota(jnp.int32, (128, 128), 0) == lax.broadcasted_iota(jnp.int32, (128, 128), 1), ridge, 0.0
    ).astype(F32)
    for t, (i, j) in enumerate(TRI):
        blk = g_ref[t * 128 : (t + 1) * 128, :] / total
        if i == j:
            blk = blk + eye
        ri, rj = slice(i * 128, (i + 1) * 128), slice(j * 128, (j + 1) * 128)
        hi_ref[ri, rj], lo_ref[ri, rj], lo2_ref[ri, rj] = split3(blk)
        if i != j:
            hi_ref[rj, ri], lo_ref[rj, ri], lo2_ref[rj, ri] = split3(blk.T)
    for i in range(NB):
        blk = g_ref[XY0 + i * 128 : XY0 + (i + 1) * 128, :].T / total
        b_ref[i * 128 : (i + 1) * 128, :] = jnp.where(lane < BINS, blk, 0.0)
    b = b_ref[...]
    r_ref[...] = b
    x_ref[...] = jnp.zeros((C, 128), F32)
    bb = col_sum(b * b)
    safe_bb = jnp.where(bb > 0, bb, 1.0)

    def inner_cond(s):
        return (s[1] > 1.0) & (s[0] < 2000)

    def rounds_cond(s):
        return (s[1] > 1.0) & (s[0] < 40)

    def rounds(s):
        n, worst = s
        r = r_ref[...]
        rr0 = col_sum(r * r)
        goal = jnp.maximum(rr0 * INNER2, bb * FINAL2 * 0.25)
        goal = jnp.where(goal > 0, goal, 1.0)
        d_ref[...] = jnp.zeros((C, 128), F32)
        p_ref[...] = r

        def inner(t):
            it, _, rr = t
            p = p_ref[...]
            hi, lo = split(p)
            cat_ref[:, :128] = hi
            cat_ref[:, 128:] = lo
            cat = cat_ref[...]
            pap = jnp.zeros((1, 128), F32)
            for m in range(2):
                rows = slice(m * 384, (m + 1) * 384)
                q = jnp.dot(hi_ref[rows, :], cat, preferred_element_type=F32) + jnp.dot(
                    lo_ref[rows, :], cat, preferred_element_type=F32
                )
                q = q[:, :128] + q[:, 128:]
                q_ref[rows, :] = q
                pap = pap + col_sum(q * p_ref[rows, :])
            alpha = jnp.where(pap > 0, rr / jnp.where(pap > 0, pap, 1.0), 0.0)
            r = r_ref[...] - alpha * q_ref[...]
            r_ref[...] = r
            d_ref[...] = d_ref[...] + alpha * p
            new = col_sum(r * r)
            beta = jnp.where(rr > 0, new / jnp.where(rr > 0, rr, 1.0), 0.0)
            p_ref[...] = r + beta * p
            return it + 1, jnp.max(new / goal), new

        lax.while_loop(inner_cond, inner, (jnp.int32(0), jnp.float32(2.0), rr0))
        x = x_ref[...] + d_ref[...]
        x_ref[...] = x
        hi, lo, lo2 = split3(x)
        cat_ref[:, :128] = hi
        cat_ref[:, 128:] = lo
        cat = cat_ref[...]
        for m in range(3):
            rows = slice(m * 256, (m + 1) * 256)
            q = jnp.dot(lo2_ref[rows, :], cat, preferred_element_type=F32)
            q = q + jnp.dot(lo_ref[rows, :], cat, preferred_element_type=F32)
            q = q + jnp.dot(hi_ref[rows, :], cat, preferred_element_type=F32)
            q_ref[rows, :] = q[:, :128] + (
                q[:, 128:] + jnp.dot(hi_ref[rows, :], lo2, preferred_element_type=F32)
            )
        r = b_ref[...] - q_ref[...]
        r_ref[...] = r
        now = jnp.max(col_sum(r * r) / (safe_bb * FINAL2))
        go = (now > 1.0) & (now < 0.25 * worst)
        return n + 1, jnp.where(go, now, 0.0)

    lax.while_loop(rounds_cond, rounds, (jnp.int32(0), jnp.float32(3.0e38)))
    scale = jnp.sqrt(jnp.full((1, 128), total * BINS, F32))
    out_ref[...] = (x_ref[...] * scale)[:, :BINS]


INNER2 = 1e-8
FINAL2 = 1e-12


def solve(packed):
    mat = pltpu.VMEM((C, 128), F32)
    return pl.pallas_call(
        solve_kernel,
        out_shape=jax.ShapeDtypeStruct((C, BINS), F32),
        in_specs=[VMEM],
        out_specs=VMEM,
        scratch_shapes=[
            pltpu.VMEM((C, C), BF),
            pltpu.VMEM((C, C), BF),
            pltpu.VMEM((C, C), BF),
            mat, mat, mat, mat, mat, mat,
            pltpu.VMEM((C, 256), BF),
        ],
        compiler_params=pltpu.CompilerParams(vmem_limit_bytes=48 * 1024 * 1024),
        name="ridge_solve",
    )(packed)


W = 240
HID = 3072
NJ = W // 8
PJ = NJ + 6
PIX = 1024


def orders():
    p = lax.broadcasted_iota(jnp.int32, (PJ * 8, W), 0)
    w = lax.broadcasted_iota(jnp.int32, (PJ * 8, W), 1)
    spread = (w == (p % 8) * NJ + p // 8 - 3).astype(BF)
    w = lax.broadcasted_iota(jnp.int32, (W, W), 0)
    p = lax.broadcasted_iota(jnp.int32, (W, W), 1)
    back = (w == (p % 8) * NJ + p // 8).astype(BF)
    return spread, back


ATANH_ERF = [0.7978842690838895, 0.03633414661429164, -3.302471253972585e-05, -5.527399961498717e-05, 3.974156182767768e-06, -1.3378855696121708e-07, 1.814048873178476e-09]


def gelu_half(half):
    sq = half * half
    poly = ATANH_ERF[-1] * 2.0 * 4.0 ** (len(ATANH_ERF) - 1)
    for k in range(len(ATANH_ERF) - 2, -1, -1):
        poly = poly * sq + ATANH_ERF[k] * 2.0 * 4.0**k
    return half + half * jnp.tanh(half * poly)


def spread_weights(dw, dwb):
    for k in range(49):
        dwb[k] = jnp.broadcast_to(dw[k : k + 1, :], (8, C))


def add_rows(xs, dwb, sums, at, lanes, rows):
    for slot, r in rows:
        x = xs[slot, pl.ds(at, 12), :, lanes]
        for b in range(7):
            xb = x[b : b + 6]
            for h in range(4):
                if 0 <= r - h < 7:
                    sums[h] = sums[h] + xb * dwb[(r - h) * 7 + b, :, lanes][None]
    return sums


OWN_ROWS = [(k, 3 + k) for k in range(4)]
HALO_ROWS = [(k, k if k < 3 else 4 + k) for k in range(6)]


def bring_row(r, xin, xs, spread):
    xs[r] = jnp.dot(spread[...], xin[r], preferred_element_type=F32).reshape(PJ, 8, C)


def own_kernel(own, dw, vec, spread, acc, was, xin, xs, dwb, sems):
    copy = pltpu.make_async_copy(own, xin, sems.at[0])
    copy.start()
    spread_weights(dw, dwb)
    copy.wait()

    def bring(r, _):
        bring_row(r, xin, xs, spread)
        was[pl.ds(pl.multiple_of(r * W, W), W), :] = xs[r, 3 : 3 + NJ].reshape(W, C).astype(BF)
        return 0

    lax.fori_loop(0, 4, bring, 0)

    def conv(t, _):
        lanes = pl.ds(pl.multiple_of((t // 5) * 128, 128), 128)
        at = (t % 5) * 6
        bias = jnp.broadcast_to(vec[0:1, lanes], (6, 8, 128))
        sums = add_rows(xs, dwb, [bias, bias, bias, bias], at, lanes, OWN_ROWS)
        for h in range(4):
            acc[h, pl.ds(at, 6), :, lanes] = sums[h]
        return 0

    lax.fori_loop(0, 30, conv, 0)


def block_kernel(
    part, was_in, top, bot, dw, vec, b_in, spread, back, bins, counts, w_in, w_out,
    feat, packed,
    xin, xs, dwb, acc, was, normed, hid, f_ref, odd, even, win, wout, fout, sems,
):
    copies = [
        pltpu.make_async_copy(top, xin.at[pl.ds(0, 3)], sems.at[0]),
        pltpu.make_async_copy(bot, xin.at[pl.ds(3, 3)], sems.at[1]),
        pltpu.make_async_copy(part, acc, sems.at[2]),
        pltpu.make_async_copy(w_in, win, sems.at[3]),
        pltpu.make_async_copy(w_out, wout, sems.at[4]),
        pltpu.make_async_copy(was_in, was, sems.at[5]),
    ]
    for copy in copies:
        copy.start()
    spread_weights(dw, dwb)
    for copy in copies[:2]:
        copy.wait()

    def bring(r, _):
        bring_row(r, xin, xs, spread)
        return 0

    lax.fori_loop(0, 6, bring, 0)
    copies[2].wait()

    def conv(t, _):
        lanes = pl.ds(pl.multiple_of((t // 5) * 128, 128), 128)
        at = (t % 5) * 6
        sums = [acc[h, pl.ds(at, 6), :, lanes] for h in range(4)]
        sums = add_rows(xs, dwb, sums, at, lanes, HALO_ROWS)
        for h in range(4):
            acc[h, pl.ds(at, 6), :, lanes] = sums[h]
        return 0

    lax.fori_loop(0, 30, conv, 0)

    def norm(h, _):
        v = acc[h].reshape(W, C)
        mean = jnp.mean(v, axis=1, keepdims=True)
        v = v - mean
        var = jnp.mean(v * v, axis=1, keepdims=True)
        v = v * lax.rsqrt(var + 1e-06) * vec[1:2, :] + vec[2:3, :]
        normed[pl.ds(pl.multiple_of(h * W, W), W), :] = v.astype(BF)
        return 0

    lax.fori_loop(0, 4, norm, 0)
    copies[3].wait()

    def up(n, _):
        cols = pl.ds(pl.multiple_of(n * 256, 256), 256)
        h = jnp.dot(normed[...], win[:, cols], preferred_element_type=F32) + b_in[:, cols]
        hid[:, cols] = gelu_half(h).astype(BF)
        return 0

    lax.fori_loop(0, HID // 256, up, 0)
    copies[4].wait()
    copies[5].wait()
    f_ref[4 * W :, :] = jnp.zeros((PIX - 4 * W, C), BF)

    def down(n, _):
        cols = pl.ds(pl.multiple_of(n * 256, 256), 256)
        branch = jnp.dot(hid[...], wout[:, cols], preferred_element_type=F32) + vec[3:4, cols]
        f_ref[: 4 * W, cols] = (was[:, cols].astype(F32) + vec[4:5, cols] * branch).astype(BF)
        return 0

    lax.fori_loop(0, C // 256, down, 0)

    def order(m, _):
        rows = pl.ds(pl.multiple_of(m * W, W), W)
        fout[m] = jnp.dot(back[...], f_ref[rows, :], preferred_element_type=F32).astype(BF)
        return 0

    lax.fori_loop(0, 4, order, 0)
    leave = pltpu.make_async_copy(fout, feat, sems.at[6])
    leave.start()

    weight = jnp.where(bins[...] >= 0, counts[...], 0)
    odd_w = weight % 2
    even_w = (weight - odd_w).astype(F32)
    odd_w = odd_w.astype(F32)
    for i in range(NB):
        flip = f_ref[:, i * 128 : (i + 1) * 128].astype(F32).T
        odd[...] = (flip * odd_w).astype(BF)
        even[...] = (flip * even_w).astype(BF)
        side = f_ref[:, i * 128 :]
        gram = jnp.dot(odd[...], side, preferred_element_type=F32) + jnp.dot(
            even[...], side, preferred_element_type=F32
        )
        for j in range(i, NB):
            t = TRI.index((i, j))
            packed[t * 128 : (t + 1) * 128, :] = gram[:, (j - i) * 128 : (j - i + 1) * 128]
    hot = lax.broadcasted_iota(jnp.int32, (128, PIX), 0) == bins[...]
    hot = jnp.where(hot, weight, 0).astype(F32).astype(BF)
    xy = jnp.dot(hot, f_ref[...], preferred_element_type=F32)
    total = jnp.sum(weight.astype(F32), axis=1, keepdims=True)
    xy = jnp.where(lax.broadcasted_iota(jnp.int32, (128, C), 0) == BINS, total, xy)
    for i in range(NB):
        packed[XY0 + i * 128 : XY0 + (i + 1) * 128, :] = xy[:, i * 128 : (i + 1) * 128]
    packed[ROWS:, :] = jnp.zeros((PACK - ROWS, 128), F32)
    leave.wait()


def run_own(own, dw, vec, spread):
    part = jax.ShapeDtypeStruct((4, NJ, 8, C), F32)
    was = jax.ShapeDtypeStruct((4 * W, C), BF)
    return pl.pallas_call(
        own_kernel,
        out_shape=(part, was),
        in_specs=[pl.BlockSpec(memory_space=pl.ANY)] + [VMEM] * 3,
        out_specs=(VMEM, VMEM),
        scratch_shapes=[
            pltpu.VMEM((4, W, C), BF),
            pltpu.VMEM((4, PJ, 8, C), F32),
            pltpu.VMEM((49, 8, C), F32),
            pltpu.SemaphoreType.DMA((1,)),
        ],
        compiler_params=pltpu.CompilerParams(vmem_limit_bytes=24 * 1024 * 1024),
        cost_estimate=pl.CostEstimate(flops=6_000_000_000, bytes_accessed=12_000_000, transcendentals=0),
        name="own_rows",
    )(own, dw, vec, spread)


def run_block(own, top, bot, dw, vec, b_in, bins, counts, w_in, w_out):
    spread, back = orders()
    part, was = run_own(own, dw, vec, spread)
    anyspec = pl.BlockSpec(memory_space=pl.ANY)
    return pl.pallas_call(
        block_kernel,
        out_shape=(jax.ShapeDtypeStruct(own.shape, BF), jax.ShapeDtypeStruct((PACK, 128), F32)),
        in_specs=[anyspec] * 4 + [VMEM] * 7 + [anyspec] * 2,
        out_specs=(anyspec, VMEM),
        scratch_shapes=[
            pltpu.VMEM((6, W, C), BF),
            pltpu.VMEM((6, PJ, 8, C), F32),
            pltpu.VMEM((49, 8, C), F32),
            pltpu.VMEM((4, NJ, 8, C), F32),
            pltpu.VMEM((4 * W, C), BF),
            pltpu.VMEM((4 * W, C), BF),
            pltpu.VMEM((4 * W, HID), BF),
            pltpu.VMEM((PIX, C), BF),
            pltpu.VMEM((128, PIX), BF),
            pltpu.VMEM((128, PIX), BF),
            pltpu.VMEM((C, HID), BF),
            pltpu.VMEM((HID, C), BF),
            pltpu.VMEM((4, W, C), BF),
            pltpu.SemaphoreType.DMA((7,)),
        ],
        compiler_params=pltpu.CompilerParams(vmem_limit_bytes=48 * 1024 * 1024),
        name="block",
    )(part, was, top, bot, dw, vec, b_in, spread, back, bins, counts, w_in, w_out)


def pixel_row(arr, fill):
    arr = arr.reshape(4, 8, NJ).transpose(0, 2, 1).reshape(1, 4 * W)
    return jnp.pad(arr, ((0, 0), (0, PIX - 4 * W)), constant_values=fill)


def per_device(
    frames_in, dw_weight, dw_bias, ln_gain, ln_bias, w_in, b_in, w_out, b_out, layer_scale, depth_bins, return_counts
):
    own = frames_in[0]
    ends = lax.axis_size("strip") - 1
    bot = lax.ppermute(own[:3], "strip", [(i + 1, i) for i in range(ends)])
    top = lax.ppermute(lax.optimization_barrier(own)[1:], "strip", [(i, i + 1) for i in range(ends)])
    vec = jnp.stack([dw_bias, 0.5 * ln_gain, 0.5 * ln_bias, b_out, layer_scale, b_out, b_out, b_out])
    features, packed = run_block(
        own, top, bot, dw_weight.reshape(49, C), vec, 0.5 * b_in.reshape(1, HID),
        pixel_row(depth_bins[0], -1), pixel_row(return_counts[0], 0), w_in, w_out,
    )
    return (features[None], solve(sum_devices(packed)))


def solution(mesh):
    placed = (
        P("frame", "strip", None, None),
        P(),
        P(),
        P(),
        P(),
        P(),
        P(),
        P(),
        P(),
        P(),
        P("frame", "strip", None),
        P("frame", "strip", None),
    )
    return jax.shard_map(
        per_device,
        mesh=mesh,
        in_specs=placed,
        out_specs=(P("frame", "strip", None, None), P()),
        check_vma=False,
    )
```
